128 devices in a mesh: lat: 16 (over z, x), lon: 8 (over y, core).
Axes of the slice: x: 4, y: 4, z: 4, core: 2. Of those that a mesh axis runs over, the one named last changes fastest.
Arguments:
- parent: bfloat16 [256, 256, 512], P('lat', 'lon'), may hold values from -6 to 6
- diffusion: float32 [512], replicated, may hold values from 0.05 to 0.25
- nest_state: bfloat16 [32768, 8, 512], P(('lat', 'lon')), may hold values from -6 to 6
- nest_cotangent: bfloat16 [32768, 8, 512], P(('lat', 'lon')), may hold values from -6 to 6
- owner_count: int32 [128], P(('lat', 'lon')), may hold values from 0 to 256, as said below
- tile_pos: int32 [32768], P(('lat', 'lon')), may hold values from 0 to 511
- w_in: bfloat16 [512, 2048], replicated, may hold values from -0.25 to 0.25
- w_out: bfloat16 [2048, 512], replicated, may hold values from -0.125 to 0.125
Outputs:
- parent_out: bfloat16 [256, 256, 512], P('lat', 'lon')
- nest_grad: bfloat16 [32768, 8, 512], P(('lat', 'lon'))
- w_in_grad: float32 [512, 2048], replicated
- w_out_grad: float32 [2048, 512], replicated
The draws below stay inside these ranges and needn't reach their ends.
Inputs may be any that keep to these rules, and one draw needn't show every extreme that they name: `owner_count`: the counts of all devices sum to 8192; each is a multiple of 2; some device has exactly 256. Only the first count slots of a device are live; the entries of its other slots are not used.
All inputs are finite; a program needn't handle non-finite values.
Results may differ from the reference program's by a relative error of at most 0.012.
Values may be sent and summed in bfloat16 or wider, within the bound.
A program may use at most 128 MiB of HBM per device.

```python
import math
import jax
import jax.numpy as jnp
from jax import lax

C = 512
FF = 2048
BLAT = 16
BLON = 32
TILE_ROWS = 8
OWN = 256
NLAT = 256
NLON = 256
TILES = 32768
LIVE_TILES = 8192
CAP = 2
N_LON = 8


def draw_owner_count(key, part):
    devices = TILES // OWN
    half = OWN // 2
    steps_max = half // CAP
    pairs = devices // 4
    key_order = jax.random.fold_in(key, 11)
    key_extra = jax.random.fold_in(key, 23)
    order = jax.random.permutation(key_order, devices)
    extra = jax.random.randint(key_extra, (pairs,), 0, steps_max + 1)
    extra = extra.at[0].set(steps_max)
    first = half + CAP * extra
    second = half - CAP * extra
    values = jnp.concatenate([first, second, jnp.zeros((devices - 2 * pairs,), jnp.int32)]).astype(jnp.int32)
    return jnp.zeros((devices,), jnp.int32).at[order].set(values)


def with_ends(values, stream_key, smallest, largest):
    longest = values.shape.index(max(values.shape))
    spots = []
    for shift in (0, 1):
        where = [jax.random.randint(jax.random.fold_in(stream_key, axis), (), 0, length) for axis, length in enumerate(values.shape)]
        where[longest] = (where[longest] + shift) % values.shape[longest]
        spots.append(tuple(where))
    return values.at[spots[0]].set(smallest).at[spots[1]].set(largest)


def shard_levels(key, shape, split, smallest, high):
    def one(position, blocks):
        steps = jax.random.uniform(jax.random.fold_in(jax.random.fold_in(key, 6), position), (blocks,), jnp.float32, smallest / len(split), high / len(split))
        return jnp.repeat(jnp.exp(steps), shape[position] // blocks).reshape((-1,) + (1,) * (len(shape) - position - 1))

    level = one(*split[0])
    for cut in split[1:]:
        level = level * one(*cut)
    return level


def scatter_about(key, shape, deviation, limit, cuts=(), kind=jnp.bfloat16):
    loudness = shard_levels(key, shape, cuts, -0.22, 0.18) if cuts else 1.0
    drawn = jax.random.normal(key, shape, jnp.float32) * deviation * loudness
    return jnp.minimum(jnp.maximum(drawn, -limit), limit).astype(kind)


def setup_inputs(seed: int = 0) -> dict:
    seeds = jax.random.split(jax.random.key(seed), 9)
    return {
        "parent": scatter_about(seeds[0], (NLAT, NLON, C), 1.0, 6.0, ((0, 16), (1, 8))),
        "diffusion": jnp.clip(jnp.exp(jax.random.uniform(seeds[1], (C,), jnp.float32, math.log(0.05), math.log(0.25))), 0.05, 0.25),
        "nest_state": scatter_about(seeds[2], (TILES, TILE_ROWS, C), 1.0, 6.0, ((0, 128),)),
        "nest_cotangent": scatter_about(seeds[3], (TILES, TILE_ROWS, C), 1.0, 6.0, ((0, 128),)),
        "owner_count": draw_owner_count(jax.random.fold_in(seeds[8], 71), 0),
        "tile_pos": with_ends(jax.random.randint(seeds[5], (TILES,), 0, BLAT * BLON), jax.random.fold_in(seeds[5], 1), 0, (BLAT * BLON) - 1).astype(jnp.int32),
        "w_in": scatter_about(seeds[6], (C, FF), C ** -0.5, 0.25),
        "w_out": scatter_about(seeds[7], (FF, C), FF ** -0.5, 0.125),
    }


def nest_block(inputs, cotangent, w_in, w_out):
    count, cells, chans = inputs.shape
    rows = inputs.reshape(count * cells, chans)
    grads = cotangent.reshape(count * cells, chans)
    hidden = jnp.dot(rows, w_in, preferred_element_type=jnp.float32)
    active = jax.nn.gelu(hidden).astype(jnp.bfloat16)
    output = rows.astype(jnp.float32) + jnp.dot(active, w_out, preferred_element_type=jnp.float32)
    feedback = lax.optimization_barrier(jnp.mean(output.reshape(count, cells, chans), axis=1)).astype(jnp.bfloat16)
    d_active = jnp.dot(grads, w_out.T, preferred_element_type=jnp.float32)
    d_hidden = jax.vjp(jax.nn.gelu, hidden)[1](d_active)[0].astype(jnp.bfloat16)
    d_inputs = (grads.astype(jnp.float32) + jnp.dot(d_hidden, w_in.T, preferred_element_type=jnp.float32)).astype(jnp.bfloat16)
    grad_in = jnp.dot(rows.T, d_hidden, preferred_element_type=jnp.float32)
    grad_out = jnp.dot(active.T, grads, preferred_element_type=jnp.float32)
    return (d_inputs.reshape(count, cells, chans), feedback, grad_in, grad_out)

def reference(parent, diffusion, nest_state, nest_cotangent, owner_count, tile_pos, w_in, w_out):
    field = parent.astype(jnp.float32)
    lat_pad = jnp.pad(field, ((1, 1), (0, 0), (0, 0)))
    beside_all = lat_pad[2:] + lat_pad[:-2] + jnp.roll(field, 1, axis=1) + jnp.roll(field, -1, axis=1) - 4.0 * field
    smoothed = field + diffusion * beside_all
    slots = jnp.arange(TILES, dtype=jnp.int32)
    owner = (slots // OWN).astype(jnp.int32)
    local = (slots % OWN).astype(jnp.int32)
    live = local < owner_count[owner]
    lat_index = (owner // N_LON * BLAT + tile_pos // BLON).astype(jnp.int32)
    lon_index = (owner % N_LON * BLON + tile_pos % BLON).astype(jnp.int32)
    chosen = jnp.nonzero(live, size=LIVE_TILES)[0].astype(jnp.int32)
    group = 64
    blocks = chosen.reshape(LIVE_TILES // group, group)

    def one_block(carry, ids):
        context = smoothed[lat_index[ids], lon_index[ids]]
        inputs = (nest_state[ids].astype(jnp.float32) + context[:, None, :]).astype(jnp.bfloat16)
        d_inputs, feedback, grad_in, grad_out = nest_block(inputs, nest_cotangent[ids], w_in, w_out)
        return ((carry[0] + grad_in, carry[1] + grad_out), (d_inputs, feedback))
    start = (jnp.zeros((C, FF), jnp.float32), jnp.zeros((FF, C), jnp.float32))
    sums, stacked = lax.scan(one_block, start, blocks)
    d_inputs = stacked[0].reshape(LIVE_TILES, TILE_ROWS, C)
    feedback = stacked[1].reshape(LIVE_TILES, C).astype(jnp.float32)
    nest_grad = jnp.zeros((TILES, TILE_ROWS, C), jnp.bfloat16).at[chosen].set(d_inputs)
    summed = jnp.zeros((NLAT, NLON, C), jnp.float32).at[lat_index[chosen], lon_index[chosen]].add(feedback)
    parent_out = (smoothed + summed).astype(jnp.bfloat16)
    factor = 1.0 / math.sqrt(LIVE_TILES * TILE_ROWS)
    return (parent_out, nest_grad, sums[0] * factor, sums[1] * factor)
```

```python
import math

import jax
import jax.numpy as jnp
from jax import lax
from jax.experimental import pallas as pl
from jax.experimental.pallas import tpu as pltpu
from jax.sharding import PartitionSpec as P

MESH = pl.DeviceIdType.MESH
F32 = jnp.float32
BF16 = jnp.bfloat16
NT = (((1,), (1,)), ((), ()))
TN = (((0,), (0,)), ((), ()))
G0 = math.sqrt(2.0 / math.pi)
G1 = G0 * 0.044715
CH = 256
NCH = 8
VMEM = pl.BlockSpec(memory_space=pltpu.VMEM)
PLANE = [(a, b) for a in range(4) for b in range(4) if a or b]


def extended(x, sides, width, wrap):
    for axis, dim in sides:
        size, length = (lax.axis_size(axis), x.shape[dim])
        up = [(i, (i + 1) % size) for i in range(size if wrap else size - 1)]
        down = [(j, i) for i, j in up]
        last = lax.slice_in_dim(x, length - width, length, axis=dim)
        leading = lax.slice_in_dim(x, 0, width, axis=dim)
        before = lax.ppermute(last, axis, up)
        after = lax.ppermute(leading, axis, down)
        x = jnp.concatenate([before, x, after], axis=dim)
    return x


def gelu_pair(h, da):
    h2 = h * h
    s = 0.5 + 0.5 * jnp.tanh(h * (G0 + G1 * h2))
    act = h * s
    slope = s + act * (1.0 - s) * (2.0 * G0 + 6.0 * G1 * h2)
    return act.astype(BF16), (slope * da).astype(BF16)


def block_kernel(factor, x, cot, wi, wo, part, dx, fb, xT, act, dh):
    xT[...] = x[...].T

    def chunk(j, carry):
        cols = pl.ds(pl.multiple_of(j * CH, CH), CH)

        def tile(r, carry):
            rows = pl.ds(pl.multiple_of(r * 512, 512), 512)
            h = jnp.dot(x[rows, :], wi[:, cols], preferred_element_type=F32)
            da = lax.dot_general(cot[rows, :], wo[cols, :], NT, preferred_element_type=F32)
            a, d = gelu_pair(h, da)
            act[rows, cols] = a
            dh[rows, cols] = d
            return carry

        lax.fori_loop(0, 4, tile, 0)
        gi = jnp.dot(xT[...], dh[:, cols], preferred_element_type=F32) * factor
        for k in range(2):
            part[j, 0, 32 * k : 32 * k + 32] = gi[:, 128 * k : 128 * k + 128].astype(BF16).reshape(32, 16, 128)
        go = lax.dot_general(act[:, cols], cot[...], TN, preferred_element_type=F32) * factor
        for k in range(4):
            part[j, 1, 16 * k : 16 * k + 16] = go[:, 128 * k : 128 * k + 128].astype(BF16).reshape(16, 16, 128)
        return carry

    lax.fori_loop(0, NCH, chunk, 0)

    def rest(r, carry):
        rows = pl.ds(pl.multiple_of(r * 256, 256), 256)
        d = lax.dot_general(dh[rows, :], wi[...], NT, preferred_element_type=F32)
        dx[rows, :] = (d + cot[rows, :].astype(F32)).astype(BF16)
        o = jnp.dot(act[rows, :], wo[...], preferred_element_type=F32) + x[rows, :].astype(F32)
        fb[pl.ds(pl.multiple_of(r * 32, 32), 32), :] = jnp.mean(o.reshape(32, 8, 512), axis=1).astype(BF16)
        return carry

    lax.fori_loop(0, 8, rest, 0)


class Place:
    def __init__(self):
        a, b = lax.axis_index("lat"), lax.axis_index("lon")
        self.x, self.y, self.z = lax.rem(a, 4), b // 2, a // 4
        self.core = lax.rem(b, 2)

    def to(self, dx, dy, dz):
        x, y, z = lax.rem(self.x + dx, 4), lax.rem(self.y + dy, 4), lax.rem(self.z + dz, 4)
        return (z * 4 + x, y * 2 + self.core)

    def partner(self):
        return (self.z * 4 + self.x, self.y * 2 + 1 - self.core)

    def axis(self, a):
        ex, ez = (2 - a) // 2, a // 2
        ey = 1 - ex - ez
        return ((ex, ey, ez), self.x * ex + self.y * ey + self.z * ez)


class Reduce:
    def __init__(self, part, full, rc, half, ra, qb, rp, send, recv):
        self.part, self.full, self.rc, self.half = part, full, rc, half
        self.ra, self.qb, self.rp, self.send, self.recv = ra, qb, rp, send, recv
        self.at = Place()

    def sets(self, c):
        a0 = lax.rem(c, 3)
        (e0, q) = self.at.axis(a0)
        (e1, u) = self.at.axis(lax.rem(a0 + 1, 3))
        (e2, v) = self.at.axis(lax.rem(a0 + 2, 3))
        return e0, e1, e2, q, u, v

    def copy(self, src, dst, stage, c, device):
        pltpu.make_async_remote_copy(
            src_ref=src, dst_ref=dst, send_sem=self.send.at[stage, c], recv_sem=self.recv.at[stage, c],
            device_id=device, device_id_type=MESH,
        ).start()

    def wait(self, ref, stage, c):
        pltpu.make_async_copy(ref, ref, self.recv.at[stage, c]).wait()

    def greet(self):
        barrier = pltpu.get_barrier_semaphore()
        n = 1
        pl.semaphore_signal(barrier, inc=1, device_id=self.at.partner(), device_id_type=MESH)
        for dx in range(4):
            for dy in range(4):
                for dz in range(4):
                    if (dx or dy or dz) and not (dx and dy and dz):
                        pl.semaphore_signal(barrier, inc=1, device_id=self.at.to(dx, dy, dz), device_id_type=MESH)
                        n += 1
        pl.semaphore_wait(barrier, n)

    def s0(self, c):
        self.copy(self.part.at[c, 1 - self.at.core], self.rc.at[c], 0, c, self.at.partner())

    def s1(self, c):
        e0, e1, e2, q, u, v = self.sets(c)
        self.wait(self.rc.at[c], 0, c)
        self.half[c] = (self.part[c, self.at.core].astype(F32) + self.rc[c].astype(F32)).astype(BF16)
        for d in (1, 2, 3):
            to = lax.rem(q + d, 4)
            self.copy(self.half.at[c, pl.ds(to * 16, 16)], self.ra.at[c, d - 1], 1, c, self.at.to(*(d * e for e in e0)))

    def s2(self, c):
        e0, e1, e2, q, u, v = self.sets(c)
        self.wait(self.ra.at[c], 1, c)
        mine = pl.ds(q * 16, 16)
        total = self.part[c, self.at.core, mine].astype(F32) + self.rc[c, mine].astype(F32)
        for d in range(3):
            total += self.ra[c, d].astype(F32)
        self.qb[c] = total.astype(BF16)
        for o, (d1, d2) in enumerate(PLANE):
            to = lax.rem(u + d1, 4) * 4 + lax.rem(v + d2, 4)
            self.copy(self.qb.at[c, to], self.rp.at[c, o], 2, c, self.at.to(*(d1 * f + d2 * g for f, g in zip(e1, e2))))

    def s3(self, c):
        e0, e1, e2, q, u, v = self.sets(c)
        self.wait(self.rp.at[c], 2, c)
        total = self.qb[c, u * 4 + v].astype(F32)
        for o in range(15):
            total += self.rp[c, o].astype(F32)
        spot = self.full.at[c, self.at.core, q * 16 + u * 4 + v]
        spot[...] = total.astype(BF16)
        for d1, d2 in PLANE:
            self.copy(spot, spot, 3, c, self.at.to(*(d1 * f + d2 * g for f, g in zip(e1, e2))))

    def s4(self, c):
        e0, e1, e2, q, u, v = self.sets(c)
        self.wait(self.rp.at[c], 3, c)
        spot = self.full.at[c, self.at.core, pl.ds(q * 16, 16)]
        for d in (1, 2, 3):
            self.copy(spot, spot, 4, c, self.at.to(*(d * e for e in e0)))

    def s5(self, c):
        self.wait(self.ra.at[c], 4, c)
        spot = self.full.at[c, self.at.core]
        self.copy(spot, spot, 5, c, self.at.partner())

    def s6(self, c, gi, go):
        self.wait(self.full.at[c, 1 - self.at.core], 5, c)
        for k in range(2):
            cols = pl.ds(pl.multiple_of(c * CH + 128 * k, 128), 128)
            gi[:, cols] = self.full[c, 0, 32 * k : 32 * k + 32].reshape(512, 128)
        for k in range(4):
            rows = pl.ds(pl.multiple_of(c * CH, CH), CH)
            go[rows, 128 * k : 128 * k + 128] = self.full[c, 1, 16 * k : 16 * k + 16].reshape(256, 128)

    def drain(self, c):
        for stage, ref in enumerate((self.rc, self.ra, self.rp, self.rp, self.ra, self.rc)):
            pltpu.make_async_copy(ref.at[c], ref.at[c], self.send.at[stage, c]).wait()


def reduce_kernel(part, gi, go, *scratch):
    r = Reduce(part, *scratch)
    r.greet()
    for stage in (r.s0, r.s1, r.s2, r.s3, r.s4, r.s5, lambda c: r.s6(c, gi, go), r.drain):
        def body(c, carry, stage=stage):
            stage(c)
            return carry
        lax.fori_loop(0, NCH, body, 0)


def local(parent, diffusion, nest_state, nest_cotangent, owner_count, tile_pos, w_in, w_out):
    blat, blon, chans = parent.shape
    own_tiles, tile_rows = (nest_state.shape[0], nest_state.shape[1])
    rows = own_tiles * tile_rows
    hidden = w_in.shape[1]
    lat_pad = extended(parent, (("lat", 0),), 1, False).astype(F32)
    lon_pad = extended(parent, (("lon", 1),), 1, True).astype(F32)
    field = parent.astype(F32)
    beside_all = lat_pad[2:] + lat_pad[:-2] + lon_pad[:, 2:] + lon_pad[:, :-2] - 4.0 * field
    smoothed = field + diffusion * beside_all
    flat = smoothed.reshape(blat * blon, chans)
    context = jnp.take(flat, tile_pos, axis=0)
    inputs = (nest_state.astype(F32) + context[:, None, :]).astype(BF16).reshape(rows, chans)
    live = lax.iota(jnp.int32, own_tiles) < owner_count[0]
    cotangent = jnp.where(live[:, None, None], nest_cotangent, jnp.zeros_like(nest_cotangent)).reshape(rows, chans)
    devices = lax.axis_size(("lat", "lon"))
    factor = 1.0 / math.sqrt(own_tiles * devices // 4 * tile_rows)
    part, d_inputs, feedback = pl.pallas_call(
        lambda *refs: block_kernel(factor, *refs),
        out_shape=[
            jax.ShapeDtypeStruct((NCH, 2, 64, 16, 128), BF16),
            jax.ShapeDtypeStruct((rows, chans), BF16),
            jax.ShapeDtypeStruct((own_tiles, chans), BF16),
        ],
        in_specs=[VMEM] * 4,
        out_specs=[VMEM] * 3,
        scratch_shapes=[pltpu.VMEM((chans, rows), BF16), pltpu.VMEM((rows, hidden), BF16), pltpu.VMEM((rows, hidden), BF16)],
        compiler_params=pltpu.CompilerParams(vmem_limit_bytes=56 * 2**20),
        name="nest_block",
    )(inputs, cotangent, w_in, w_out)
    nest_grad = jnp.where(live[:, None, None], d_inputs.reshape(nest_state.shape), jnp.zeros_like(nest_state))
    onehot = ((tile_pos[:, None] == lax.iota(jnp.int32, blat * blon)[None, :]) & live[:, None]).astype(BF16)
    summed = jnp.dot(onehot.T, feedback, preferred_element_type=F32)
    parent_out = (smoothed + summed.reshape(blat, blon, chans)).astype(BF16)
    grad_in, grad_out = pl.pallas_call(
        reduce_kernel,
        out_shape=[jax.ShapeDtypeStruct(w_in.shape, BF16), jax.ShapeDtypeStruct(w_out.shape, BF16)],
        in_specs=[VMEM],
        out_specs=[VMEM] * 2,
        scratch_shapes=[
            pltpu.VMEM((NCH, 2, 64, 16, 128), BF16),
            pltpu.VMEM((NCH, 64, 16, 128), BF16),
            pltpu.VMEM((NCH, 64, 16, 128), BF16),
            pltpu.VMEM((NCH, 3, 16, 16, 128), BF16),
            pltpu.VMEM((NCH, 16, 16, 128), BF16),
            pltpu.VMEM((NCH, 15, 16, 128), BF16),
            pltpu.SemaphoreType.DMA((6, NCH)),
            pltpu.SemaphoreType.DMA((6, NCH)),
        ],
        compiler_params=pltpu.CompilerParams(collective_id=0, has_side_effects=True, vmem_limit_bytes=56 * 2**20),
        name="reduce_all",
    )(part)
    return (parent_out, nest_grad, grad_in.astype(F32), grad_out.astype(F32))


def solution(mesh):
    in_specs = (
        P("lat", "lon", None),
        P(),
        P(("lat", "lon"), None, None),
        P(("lat", "lon"), None, None),
        P(("lat", "lon")),
        P(("lat", "lon")),
        P(),
        P(),
    )
    out_specs = (P("lat", "lon", None), P(("lat", "lon"), None, None), P(), P())
    return jax.shard_map(local, mesh=mesh, in_specs=in_specs, out_specs=out_specs, check_vma=False)
```

```python
import math

import jax
import jax.numpy as jnp
from jax import lax
from jax.experimental import pallas as pl
from jax.experimental.pallas import tpu as pltpu
from jax.sharding import PartitionSpec as P

MESH = pl.DeviceIdType.MESH
F32 = jnp.float32
BF16 = jnp.bfloat16
NT = (((1,), (1,)), ((), ()))
TN = (((0,), (0,)), ((), ()))
G0 = math.sqrt(2.0 / math.pi)
G1 = G0 * 0.044715
CH = 256
NCH = 8
VMEM = pl.BlockSpec(memory_space=pltpu.VMEM)
PLANE = [(a, b) for a in range(4) for b in range(4) if a or b]


def gelu_pair(h, da):
    h2 = h * h
    s = 0.5 + 0.5 * jnp.tanh(h * (G0 + G1 * h2))
    act = h * s
    slope = s + act * (1.0 - s) * (2.0 * G0 + 6.0 * G1 * h2)
    return act.astype(BF16), (slope * da).astype(BF16)


class Place:
    def __init__(self):
        a, b = lax.axis_index("lat"), lax.axis_index("lon")
        self.x, self.y, self.z = lax.rem(a, 4), b // 2, a // 4
        self.core = lax.rem(b, 2)

    def to(self, dx, dy, dz):
        x, y, z = lax.rem(self.x + dx, 4), lax.rem(self.y + dy, 4), lax.rem(self.z + dz, 4)
        return (z * 4 + x, y * 2 + self.core)

    def partner(self):
        return (self.z * 4 + self.x, self.y * 2 + 1 - self.core)

    def side(self):
        return (self.z * 4 + self.x, lax.rem(self.y + 2 * self.core + 3, 4) * 2 + 1 - self.core)

    def lat(self, d):
        return (lax.rem(self.z * 4 + self.x + d, 16), self.y * 2 + self.core)

    def lon(self, d):
        return (self.z * 4 + self.x, lax.rem(self.y * 2 + self.core + d, 8))

    def axis(self, a):
        ex, ez = (2 - a) // 2, a // 2
        ey = 1 - ex - ez
        return ((ex, ey, ez), self.x * ex + self.y * ey + self.z * ez)


class Reduce:
    def __init__(self, part, full, rc, half, ra, qb, rp, send, recv):
        self.part, self.full, self.rc, self.half = part, full, rc, half
        self.ra, self.qb, self.rp, self.send, self.recv = ra, qb, rp, send, recv
        self.at = Place()

    def sets(self, c):
        a0 = lax.rem(c, 3)
        (e0, q) = self.at.axis(a0)
        (e1, u) = self.at.axis(lax.rem(a0 + 1, 3))
        (e2, v) = self.at.axis(lax.rem(a0 + 2, 3))
        return e0, e1, e2, q, u, v

    def copy(self, src, dst, stage, c, device):
        pltpu.make_async_remote_copy(
            src_ref=src, dst_ref=dst, send_sem=self.send.at[stage, c], recv_sem=self.recv.at[stage, c],
            device_id=device, device_id_type=MESH,
        ).start()

    def wait(self, ref, stage, c):
        pltpu.make_async_copy(ref, ref, self.recv.at[stage, c]).wait()

    def greet(self):
        barrier = pltpu.get_barrier_semaphore()
        others = [self.at.partner(), self.at.side()]
        for dx in range(4):
            for dy in range(4):
                for dz in range(4):
                    if (dx or dy or dz) and not (dx and dy and dz):
                        others.append(self.at.to(dx, dy, dz))
        for device in others:
            pl.semaphore_signal(barrier, inc=1, device_id=device, device_id_type=MESH)
        return barrier, len(others)

    def s0(self, c):
        self.copy(self.part.at[c, 1 - self.at.core], self.rc.at[c], 0, c, self.at.partner())

    def s1(self, c):
        e0, e1, e2, q, u, v = self.sets(c)
        self.wait(self.rc.at[c], 0, c)
        self.half[c] = (self.part[c, self.at.core].astype(F32) + self.rc[c].astype(F32)).astype(BF16)
        for d in (1, 2, 3):
            to = lax.rem(q + d, 4)
            self.copy(self.half.at[c, pl.ds(to * 16, 16)], self.ra.at[c, d - 1], 1, c, self.at.to(*(d * e for e in e0)))

    def s2(self, c):
        e0, e1, e2, q, u, v = self.sets(c)
        self.wait(self.ra.at[c], 1, c)
        mine = pl.ds(q * 16, 16)
        total = self.part[c, self.at.core, mine].astype(F32) + self.rc[c, mine].astype(F32)
        for d in range(3):
            total += self.ra[c, d].astype(F32)
        self.qb[c] = total.astype(BF16)
        for o, (d1, d2) in enumerate(PLANE):
            to = lax.rem(u + d1, 4) * 4 + lax.rem(v + d2, 4)
            self.copy(self.qb.at[c, to], self.rp.at[c, o], 2, c, self.at.to(*(d1 * f + d2 * g for f, g in zip(e1, e2))))

    def s3(self, c):
        e0, e1, e2, q, u, v = self.sets(c)
        self.wait(self.rp.at[c], 2, c)
        total = self.qb[c, u * 4 + v].astype(F32)
        for o in range(15):
            total += self.rp[c, o].astype(F32)
        spot = self.full.at[c, self.at.core, q * 16 + u * 4 + v]
        spot[...] = total.astype(BF16)
        for d1, d2 in PLANE:
            self.copy(spot, spot, 3, c, self.at.to(*(d1 * f + d2 * g for f, g in zip(e1, e2))))

    def s4(self, c):
        e0, e1, e2, q, u, v = self.sets(c)
        self.wait(self.rp.at[c], 3, c)
        spot = self.full.at[c, self.at.core, pl.ds(q * 16, 16)]
        for d in (1, 2, 3):
            self.copy(spot, spot, 4, c, self.at.to(*(d * e for e in e0)))

    def s5(self, c):
        self.wait(self.ra.at[c], 4, c)
        spot = self.full.at[c, self.at.core]
        self.copy(spot, spot, 5, c, self.at.partner())

    def s6(self, c, gi, go):
        self.wait(self.full.at[c, 1 - self.at.core], 5, c)
        for k in range(2):
            cols = pl.ds(pl.multiple_of(c * CH + 128 * k, 128), 128)
            gi[:, cols] = self.full[c, 0, 32 * k : 32 * k + 32].reshape(512, 128)
        for k in range(4):
            rows = pl.ds(pl.multiple_of(c * CH, CH), CH)
            go[rows, 128 * k : 128 * k + 128] = self.full[c, 1, 16 * k : 16 * k + 16].reshape(256, 128)

    def drain(self, c):
        for stage, ref in enumerate((self.rc, self.ra, self.rp, self.rp, self.ra, self.rc)):
            pltpu.make_async_copy(ref.at[c], ref.at[c], self.send.at[stage, c]).wait()


def every(n, fn):
    def body(i, carry):
        fn(i)
        return carry

    lax.fori_loop(0, n, body, 0)


def rows_of(r, n):
    return pl.ds(pl.multiple_of(r * n, n), n)


def step_kernel(
    factor, count, parent_h, diff, nest_h, cot_h, pos, wi_h, wo_h,
    pout, dx, gi, go,
    ext, edge, beside, sm, x, xT, cot, wi, wo, da, act, dh, fb, load, hs, hr, part, *scratch,
):
    r = Reduce(part, *scratch)
    at = r.at
    loads = [
        pltpu.make_async_copy(src, dst, load.at[i])
        for i, (src, dst) in enumerate(((parent_h, ext.at[pl.ds(1, 16)]), (cot_h, cot), (wo_h, wo), (nest_h, x), (wi_h, wi)))
    ]
    for c in loads:
        c.start()
    barrier, met = r.greet()
    live = count[0]

    loads[0].wait()
    for i in range(16):
        line = ext[1 + i].astype(F32)
        edge[0, i : i + 1] = line[0:1]
        edge[1, i : i + 1] = line[31:32]
    loads[1].wait()

    def mask(t):
        rows = rows_of(t, 256)
        index = lax.broadcasted_iota(jnp.int32, (256, 512), 0) + t * 256
        cot[rows, :] = jnp.where(index < live * 8, cot[rows, :].astype(F32), 0.0).astype(BF16)

    every(8, mask)
    pl.semaphore_wait(barrier, met)

    def halo(i, src, dst, device):
        c = pltpu.make_async_remote_copy(
            src_ref=src, dst_ref=dst, send_sem=hs.at[i], recv_sem=hr.at[i], device_id=device, device_id_type=MESH
        )
        c.start()
        return c

    halos = [
        halo(0, ext.at[16], ext.at[0], at.lat(1)),
        halo(1, ext.at[1], ext.at[17], at.lat(15)),
        halo(2, edge.at[1], beside.at[0], at.lon(1)),
        halo(3, edge.at[0], beside.at[1], at.lon(7)),
    ]
    loads[2].wait()

    def first_da(t):
        rows = rows_of(t, 512)
        da[rows, :] = lax.dot_general(cot[rows, :], wo[pl.ds(0, CH), :], NT, preferred_element_type=F32)

    every(4, first_da)
    cells = lax.broadcasted_iota(jnp.int32, (512, 256), 0)
    slots = lax.broadcasted_iota(jnp.int32, (512, 256), 1)
    hot = jnp.where((cells == pos[...]) & (slots < live), 1.0, 0.0).astype(BF16)
    for c in halos:
        c.wait()

    band = lax.axis_index("lat")

    @pl.when(band == 0)
    def _():
        ext[0] = jnp.zeros_like(ext[0])

    @pl.when(band == 15)
    def _():
        ext[17] = jnp.zeros_like(ext[17])

    west, east = beside[0], beside[1]
    column = lax.broadcasted_iota(jnp.int32, (32, 512), 0)
    rate = diff[...]
    for i in range(16):
        f = ext[1 + i].astype(F32)
        w = jnp.where(column == 0, west[i : i + 1], pltpu.roll(f, 1, 0))
        e = jnp.where(column == 31, east[i : i + 1], pltpu.roll(f, 31, 0))
        near = ext[i].astype(F32) + ext[2 + i].astype(F32) + w + e - 4.0 * f
        sm[32 * i : 32 * i + 32] = f + rate * near
    field = sm[...]
    high = field.astype(BF16)
    low = (field - high.astype(F32)).astype(BF16)
    context = lax.dot_general(hot, high, TN, preferred_element_type=F32)
    context += lax.dot_general(hot, low, TN, preferred_element_type=F32)
    loads[3].wait()
    for t in range(4):
        rows = pl.ds(t * 512, 512)
        wide = jnp.broadcast_to(context[64 * t : 64 * t + 64, None, :], (64, 8, 512)).reshape(512, 512)
        x[rows, :] = (x[rows, :].astype(F32) + wide).astype(BF16)
    loads[4].wait()
    xT[...] = x[...].T

    def tiles(j, first):
        cols = rows_of(j, CH)

        def tile(t):
            rows = rows_of(t, 512)
            h = jnp.dot(x[rows, :], wi[:, cols], preferred_element_type=F32)
            if first:
                d = da[rows, :]
            else:
                d = lax.dot_general(cot[rows, :], wo[cols, :], NT, preferred_element_type=F32)
            a, d = gelu_pair(h, d)
            act[rows, cols] = a
            dh[rows, cols] = d

        every(4, tile)

    def grads(j):
        cols = rows_of(j, CH)
        g = jnp.dot(xT[...], dh[:, cols], preferred_element_type=F32) * factor
        for k in range(2):
            part[j, 0, 32 * k : 32 * k + 32] = g[:, 128 * k : 128 * k + 128].astype(BF16).reshape(32, 16, 128)
        g = lax.dot_general(act[:, cols], cot[...], TN, preferred_element_type=F32) * factor
        for k in range(4):
            part[j, 1, 16 * k : 16 * k + 16] = g[:, 128 * k : 128 * k + 128].astype(BF16).reshape(16, 16, 128)

    def rest(t):
        rows = rows_of(t, 256)
        d = lax.dot_general(dh[rows, :], wi[...], NT, preferred_element_type=F32)
        dx[rows, :] = (d + cot[rows, :].astype(F32)).astype(BF16)
        o = jnp.dot(act[rows, :], wo[...], preferred_element_type=F32) + x[rows, :].astype(F32)
        fb[rows_of(t, 32), :] = jnp.mean(o.reshape(32, 8, 512), axis=1).astype(BF16)

    def stages(s, *pairs):
        for stage, delay in pairs:
            c = s - delay

            @pl.when((c >= 0) & (c < NCH))
            def _():
                stage(c)

    odd = ((r.s1, 1), (r.s3, 4), (r.s5, 7))
    even = ((r.s2, 2), (r.s4, 5), (lambda c: r.s6(c, gi, go), 7))
    tiles(0, True)

    def slot(s):
        @pl.when(s > 0)
        def _():
            tiles(s, False)

        stages(s, *odd)
        grads(s)
        r.s0(s)
        stages(s, *even)

    every(NCH, slot)

    def late(i):
        @pl.when(i < 4)
        def _():
            rest(2 * i)

        stages(i + 8, *odd)

        @pl.when(i < 4)
        def _():
            rest(2 * i + 1)

        @pl.when(i == 4)
        def _():
            pout[...] = (sm[...] + jnp.dot(hot, fb[...], preferred_element_type=F32)).astype(BF16)

        stages(i + 8, *even)

    every(7, late)
    every(NCH, r.drain)


def local(parent, diffusion, nest_state, nest_cotangent, owner_count, tile_pos, w_in, w_out):
    blat, blon, chans = parent.shape
    own_tiles, tile_rows = (nest_state.shape[0], nest_state.shape[1])
    rows, cells, hidden = own_tiles * tile_rows, blat * blon, w_in.shape[1]
    devices = lax.axis_size(("lat", "lon"))
    factor = 1.0 / math.sqrt(own_tiles * devices // 4 * tile_rows)
    hbm = pl.BlockSpec(memory_space=pl.ANY)
    parent_out, nest_grad, grad_in, grad_out = pl.pallas_call(
        lambda *refs: step_kernel(factor, *refs),
        out_shape=[
            jax.ShapeDtypeStruct((cells, chans), BF16),
            jax.ShapeDtypeStruct((rows, chans), BF16),
            jax.ShapeDtypeStruct(w_in.shape, BF16),
            jax.ShapeDtypeStruct(w_out.shape, BF16),
        ],
        in_specs=[pl.BlockSpec(memory_space=pltpu.SMEM), hbm, VMEM, hbm, hbm, VMEM, hbm, hbm],
        out_specs=[VMEM] * 4,
        scratch_shapes=[
            pltpu.VMEM((blat + 2, blon, chans), BF16),
            pltpu.VMEM((2, blat, chans), F32),
            pltpu.VMEM((2, blat, chans), F32),
            pltpu.VMEM((cells, chans), F32),
            pltpu.VMEM((rows, chans), BF16),
            pltpu.VMEM((chans, rows), BF16),
            pltpu.VMEM((rows, chans), BF16),
            pltpu.VMEM(w_in.shape, BF16),
            pltpu.VMEM(w_out.shape, BF16),
            pltpu.VMEM((rows, CH), F32),
            pltpu.VMEM((rows, hidden), BF16),
            pltpu.VMEM((rows, hidden), BF16),
            pltpu.VMEM((own_tiles, chans), BF16),
            pltpu.SemaphoreType.DMA((5,)),
            pltpu.SemaphoreType.DMA((4,)),
            pltpu.SemaphoreType.DMA((4,)),
            pltpu.VMEM((NCH, 2, 64, 16, 128), BF16),
            pltpu.VMEM((NCH, 2, 64, 16, 128), BF16),
            pltpu.VMEM((NCH, 64, 16, 128), BF16),
            pltpu.VMEM((NCH, 64, 16, 128), BF16),
            pltpu.VMEM((NCH, 3, 16, 16, 128), BF16),
            pltpu.VMEM((NCH, 16, 16, 128), BF16),
            pltpu.VMEM((NCH, 15, 16, 128), BF16),
            pltpu.SemaphoreType.DMA((6, NCH)),
            pltpu.SemaphoreType.DMA((6, NCH)),
        ],
        compiler_params=pltpu.CompilerParams(collective_id=0, has_side_effects=True, vmem_limit_bytes=60 * 2**20),
        name="nest_step",
    )(
        owner_count, parent, diffusion.reshape(1, chans), nest_state.reshape(rows, chans),
        nest_cotangent.reshape(rows, chans), tile_pos.reshape(1, own_tiles), w_in, w_out,
    )
    return (
        parent_out.reshape(parent.shape), nest_grad.reshape(nest_state.shape),
        grad_in.astype(F32), grad_out.astype(F32),
    )


def solution(mesh):
    in_specs = (
        P("lat", "lon", None),
        P(),
        P(("lat", "lon"), None, None),
        P(("lat", "lon"), None, None),
        P(("lat", "lon")),
        P(("lat", "lon")),
        P(),
        P(),
    )
    out_specs = (P("lat", "lon", None), P(("lat", "lon"), None, None), P(), P())
    return jax.shard_map(local, mesh=mesh, in_specs=in_specs, out_specs=out_specs, check_vma=False)
```

```python
import math

import jax
import jax.numpy as jnp
from jax import lax
from jax.experimental import pallas as pl
from jax.experimental.pallas import tpu as pltpu
from jax.sharding import PartitionSpec as P

MESH = pl.DeviceIdType.MESH
F32 = jnp.float32
BF16 = jnp.bfloat16
NT = (((1,), (1,)), ((), ()))
TN = (((0,), (0,)), ((), ()))
G0 = math.sqrt(2.0 / math.pi)
G1 = G0 * 0.044715
CH = 256
NCH = 8
VMEM = pl.BlockSpec(memory_space=pltpu.VMEM)
PLANE = [(a, b) for a in range(4) for b in range(4) if a or b]


def gelu_pair(h, da):
    h2 = h * h
    s = 0.5 + 0.5 * jnp.tanh(h * (G0 + G1 * h2))
    act = h * s
    slope = s + act * (1.0 - s) * (2.0 * G0 + 6.0 * G1 * h2)
    return act.astype(BF16), (slope * da).astype(BF16)


class Place:
    def __init__(self):
        a, b = lax.axis_index("lat"), lax.axis_index("lon")
        self.x, self.y, self.z = lax.rem(a, 4), b // 2, a // 4
        self.core = lax.rem(b, 2)

    def to(self, dx, dy, dz):
        x, y, z = lax.rem(self.x + dx, 4), lax.rem(self.y + dy, 4), lax.rem(self.z + dz, 4)
        return (z * 4 + x, y * 2 + self.core)

    def partner(self):
        return (self.z * 4 + self.x, self.y * 2 + 1 - self.core)

    def side(self):
        return (self.z * 4 + self.x, lax.rem(self.y + 2 * self.core + 3, 4) * 2 + 1 - self.core)

    def lat(self, d):
        return (lax.rem(self.z * 4 + self.x + d, 16), self.y * 2 + self.core)

    def lon(self, d):
        return (self.z * 4 + self.x, lax.rem(self.y * 2 + self.core + d, 8))

    def axis(self, a):
        ex, ez = (2 - a) // 2, a // 2
        ey = 1 - ex - ez
        return ((ex, ey, ez), self.x * ex + self.y * ey + self.z * ez)


class Reduce:
    def __init__(self, part, full, rc, half, ra, qb, rp, send, recv):
        self.part, self.full, self.rc, self.half = part, full, rc, half
        self.ra, self.qb, self.rp, self.send, self.recv = ra, qb, rp, send, recv
        self.at = Place()

    def sets(self, c):
        a0 = lax.rem(c, 3)
        (e0, q) = self.at.axis(a0)
        (e1, u) = self.at.axis(lax.rem(a0 + 1, 3))
        (e2, v) = self.at.axis(lax.rem(a0 + 2, 3))
        return e0, e1, e2, q, u, v

    def copy(self, src, dst, stage, c, device):
        pltpu.make_async_remote_copy(
            src_ref=src, dst_ref=dst, send_sem=self.send.at[stage, c], recv_sem=self.recv.at[stage, c],
            device_id=device, device_id_type=MESH,
        ).start()

    def wait(self, ref, stage, c):
        pltpu.make_async_copy(ref, ref, self.recv.at[stage, c]).wait()

    def greet(self):
        barrier = pltpu.get_barrier_semaphore()
        others = [self.at.partner(), self.at.side()]
        for dx in range(4):
            for dy in range(4):
                for dz in range(4):
                    if (dx or dy or dz) and not (dx and dy and dz):
                        others.append(self.at.to(dx, dy, dz))
        for device in others:
            pl.semaphore_signal(barrier, inc=1, device_id=device, device_id_type=MESH)
        return barrier, len(others)

    def s0(self, c):
        self.copy(self.part.at[c, 1 - self.at.core], self.rc.at[c], 0, c, self.at.partner())

    def s1(self, c):
        e0, e1, e2, q, u, v = self.sets(c)
        self.wait(self.rc.at[c], 0, c)
        self.half[c] = (self.part[c, self.at.core].astype(F32) + self.rc[c].astype(F32)).astype(BF16)
        for d in (1, 2, 3):
            to = lax.rem(q + d, 4)
            self.copy(self.half.at[c, pl.ds(to * 16, 16)], self.ra.at[c, d - 1], 1, c, self.at.to(*(d * e for e in e0)))

    def s2(self, c):
        e0, e1, e2, q, u, v = self.sets(c)
        self.wait(self.ra.at[c], 1, c)
        mine = pl.ds(q * 16, 16)
        total = self.part[c, self.at.core, mine].astype(F32) + self.rc[c, mine].astype(F32)
        for d in range(3):
            total += self.ra[c, d].astype(F32)
        self.qb[c] = total.astype(BF16)
        for o, (d1, d2) in enumerate(PLANE):
            to = lax.rem(u + d1, 4) * 4 + lax.rem(v + d2, 4)
            self.copy(self.qb.at[c, to], self.rp.at[c, o], 2, c, self.at.to(*(d1 * f + d2 * g for f, g in zip(e1, e2))))

    def s3(self, c):
        e0, e1, e2, q, u, v = self.sets(c)
        self.wait(self.rp.at[c], 2, c)
        total = self.qb[c, u * 4 + v].astype(F32)
        for o in range(15):
            total += self.rp[c, o].astype(F32)
        spot = self.full.at[c, self.at.core, q * 16 + u * 4 + v]
        spot[...] = total.astype(BF16)
        for d1, d2 in PLANE:
            self.copy(spot, spot, 3, c, self.at.to(*(d1 * f + d2 * g for f, g in zip(e1, e2))))

    def s4(self, c):
        e0, e1, e2, q, u, v = self.sets(c)
        self.wait(self.rp.at[c], 3, c)
        spot = self.full.at[c, self.at.core, pl.ds(q * 16, 16)]
        for d in (1, 2, 3):
            self.copy(spot, spot, 4, c, self.at.to(*(d * e for e in e0)))

    def s5(self, c):
        self.wait(self.ra.at[c], 4, c)
        spot = self.full.at[c, self.at.core]
        self.copy(spot, spot, 5, c, self.at.partner())

    def s6(self, c, sums, out):
        self.wait(self.full.at[c, 1 - self.at.core], 5, c)
        pltpu.make_async_copy(self.full.at[c], sums.at[c], out.at[c]).start()

    def drain(self, c):
        for stage, ref in enumerate((self.rc, self.ra, self.rp, self.rp, self.ra, self.rc)):
            pltpu.make_async_copy(ref.at[c], ref.at[c], self.send.at[stage, c]).wait()


def every(n, fn):
    def body(i, carry):
        fn(i)
        return carry

    lax.fori_loop(0, n, body, 0)


def rows_of(r, n):
    return pl.ds(pl.multiple_of(r * n, n), n)


def step_kernel(
    factor, count, parent_h, diff, nest_h, cot_h, pos, wi_h, wo_h,
    pout, dx, sums,
    ext, edge, beside, sm, x, xT, cot, wi, wo, da, act, dh, fb, field_out, load, out, hs, hr, part, *scratch,
):
    r = Reduce(part, *scratch)
    at = r.at
    loads = [
        pltpu.make_async_copy(src, dst, load.at[i])
        for i, (src, dst) in enumerate(((parent_h, ext.at[pl.ds(1, 16)]), (cot_h, cot), (wo_h, wo), (nest_h, x), (wi_h, wi)))
    ]
    for c in loads[:3]:
        c.start()
    barrier, met = r.greet()
    live = count[0]

    loads[0].wait()
    for i in range(16):
        line = ext[1 + i].astype(F32)
        edge[0, i : i + 1] = line[0:1]
        edge[1, i : i + 1] = line[31:32]
    pl.semaphore_wait(barrier, met)

    def halo(i, src, dst, device):
        c = pltpu.make_async_remote_copy(
            src_ref=src, dst_ref=dst, send_sem=hs.at[i], recv_sem=hr.at[i], device_id=device, device_id_type=MESH
        )
        c.start()
        return c

    halos = [
        halo(0, ext.at[16], ext.at[0], at.lat(1)),
        halo(1, ext.at[1], ext.at[17], at.lat(15)),
        halo(2, edge.at[1], beside.at[0], at.lon(1)),
        halo(3, edge.at[0], beside.at[1], at.lon(7)),
    ]
    for c in loads[3:]:
        c.start()

    def mask(t):
        rows = rows_of(t, 256)
        index = lax.broadcasted_iota(jnp.int32, (256, 512), 0) + t * 256
        cot[rows, :] = jnp.where(index < live * 8, cot[rows, :].astype(F32), 0.0).astype(BF16)

    loads[1].wait()
    every(8, mask)
    loads[2].wait()
    da[...] = lax.dot_general(cot[...], wo[pl.ds(0, CH), :], NT, preferred_element_type=F32)
    cells = lax.broadcasted_iota(jnp.int32, (512, 256), 0)
    slots = lax.broadcasted_iota(jnp.int32, (512, 256), 1)
    hot = jnp.where((cells == pos[...]) & (slots < live), 1.0, 0.0).astype(BF16)
    for c in halos:
        c.wait()

    band = lax.axis_index("lat")

    @pl.when(band == 0)
    def _():
        ext[0] = jnp.zeros_like(ext[0])

    @pl.when(band == 15)
    def _():
        ext[17] = jnp.zeros_like(ext[17])

    west, east = beside[0], beside[1]
    column = lax.broadcasted_iota(jnp.int32, (32, 512), 0)
    rate = diff[...]
    for i in range(16):
        f = ext[1 + i].astype(F32)
        w = jnp.where(column == 0, west[i : i + 1], pltpu.roll(f, 1, 0))
        e = jnp.where(column == 31, east[i : i + 1], pltpu.roll(f, 31, 0))
        near = ext[i].astype(F32) + ext[2 + i].astype(F32) + w + e - 4.0 * f
        sm[32 * i : 32 * i + 32] = f + rate * near
    field = sm[...]
    high = field.astype(BF16)
    low = (field - high.astype(F32)).astype(BF16)
    context = lax.dot_general(hot, high, TN, preferred_element_type=F32)
    context += lax.dot_general(hot, low, TN, preferred_element_type=F32)
    loads[3].wait()
    for t in range(4):
        rows = pl.ds(t * 512, 512)
        wide = jnp.broadcast_to(context[64 * t : 64 * t + 64, None, :], (64, 8, 512)).reshape(512, 512)
        x[rows, :] = (x[rows, :].astype(F32) + wide).astype(BF16)
    loads[4].wait()
    xT[...] = x[...].T

    def tiles(j, first):
        cols = rows_of(j, CH)

        h = jnp.dot(x[...], wi[:, cols], preferred_element_type=F32)
        d = da[...] if first else lax.dot_general(cot[...], wo[cols, :], NT, preferred_element_type=F32)
        a, d = gelu_pair(h, d)
        act[:, cols] = a
        dh[:, cols] = d

    def grads(j):
        cols = rows_of(j, CH)
        g = jnp.dot(xT[...], dh[:, cols], preferred_element_type=F32) * factor
        for k in range(2):
            part[j, 0, 32 * k : 32 * k + 32] = g[:, 128 * k : 128 * k + 128].astype(BF16).reshape(32, 16, 128)
        g = lax.dot_general(act[:, cols], cot[...], TN, preferred_element_type=F32) * factor
        for k in range(4):
            part[j, 1, 16 * k : 16 * k + 16] = g[:, 128 * k : 128 * k + 128].astype(BF16).reshape(16, 16, 128)

    def rest(t):
        rows = rows_of(t, 256)
        d = lax.dot_general(dh[rows, :], wi[...], NT, preferred_element_type=F32)
        cot[rows, :] = (d + cot[rows, :].astype(F32)).astype(BF16)
        pltpu.make_async_copy(cot.at[rows], dx.at[rows], out.at[t]).start()
        o = jnp.dot(act[rows, :], wo[...], preferred_element_type=F32) + x[rows, :].astype(F32)
        fb[rows_of(t, 32), :] = jnp.mean(o.reshape(32, 8, 512), axis=1).astype(BF16)

    def stages(s, *pairs):
        for stage, delay in pairs:
            c = s - delay

            @pl.when((c >= 0) & (c < NCH))
            def _():
                stage(c)

    odd = ((r.s1, 1), (r.s3, 4), (r.s5, 7),)
    even = ((r.s2, 2), (r.s4, 5), ((lambda c: r.s6(c, sums, out.at[pl.ds(8, NCH)])), 7),)
    tiles(0, True)

    def slot(s):
        @pl.when(s > 0)
        def _():
            tiles(s, False)

        stages(s, *odd)
        grads(s)
        r.s0(s)
        stages(s, *even)

    every(NCH, slot)

    def late(i):
        @pl.when(i < 4)
        def _():
            rest(2 * i)

        stages(i + 8, *odd)

        @pl.when(i < 4)
        def _():
            rest(2 * i + 1)

        @pl.when(i == 4)
        def _():
            field_out[...] = (sm[...] + jnp.dot(hot, fb[...], preferred_element_type=F32)).astype(BF16)
            pltpu.make_async_copy(field_out, pout, out.at[16]).start()

        stages(i + 8, *even)

    every(7, late)
    every(NCH, r.drain)

    def leave(t):
        rows = rows_of(t, 256)
        pltpu.make_async_copy(cot.at[rows], dx.at[rows], out.at[t]).wait()
        pltpu.make_async_copy(r.full.at[t], sums.at[t], out.at[8 + t]).wait()

    every(8, leave)
    pltpu.make_async_copy(field_out, pout, out.at[16]).wait()


def finish_kernel(sums, dx_in, field_in, gi, go, dx, field):
    for k in range(2):
        gi[:, 128 * k : 128 * k + 128] = sums[0, 0, 32 * k : 32 * k + 32].reshape(512, 128).astype(F32)
    for k in range(4):
        go[:, 128 * k : 128 * k + 128] = sums[0, 1, 16 * k : 16 * k + 16].reshape(256, 128).astype(F32)
    dx[...] = dx_in[...]
    field[...] = field_in[...]


def local(parent, diffusion, nest_state, nest_cotangent, owner_count, tile_pos, w_in, w_out):
    blat, blon, chans = parent.shape
    own_tiles, tile_rows = (nest_state.shape[0], nest_state.shape[1])
    rows, cells, hidden = own_tiles * tile_rows, blat * blon, w_in.shape[1]
    devices = lax.axis_size(("lat", "lon"))
    factor = 1.0 / math.sqrt(own_tiles * devices // 4 * tile_rows)
    hbm = pl.BlockSpec(memory_space=pl.ANY)
    parent_out, nest_grad, sums = pl.pallas_call(
        lambda *refs: step_kernel(factor, *refs),
        out_shape=[
            jax.ShapeDtypeStruct((cells, chans), BF16),
            jax.ShapeDtypeStruct((rows, chans), BF16),
            jax.ShapeDtypeStruct((NCH, 2, 64, 16, 128), BF16),
        ],
        in_specs=[pl.BlockSpec(memory_space=pltpu.SMEM), hbm, VMEM, hbm, hbm, VMEM, hbm, hbm],
        out_specs=[hbm] * 3,
        scratch_shapes=[
            pltpu.VMEM((blat + 2, blon, chans), BF16),
            pltpu.VMEM((2, blat, chans), F32),
            pltpu.VMEM((2, blat, chans), F32),
            pltpu.VMEM((cells, chans), F32),
            pltpu.VMEM((rows, chans), BF16),
            pltpu.VMEM((chans, rows), BF16),
            pltpu.VMEM((rows, chans), BF16),
            pltpu.VMEM(w_in.shape, BF16),
            pltpu.VMEM(w_out.shape, BF16),
            pltpu.VMEM((rows, CH), F32),
            pltpu.VMEM((rows, hidden), BF16),
            pltpu.VMEM((rows, hidden), BF16),
            pltpu.VMEM((own_tiles, chans), BF16),
            pltpu.VMEM((cells, chans), BF16),
            pltpu.SemaphoreType.DMA((5,)),
            pltpu.SemaphoreType.DMA((17,)),
            pltpu.SemaphoreType.DMA((4,)),
            pltpu.SemaphoreType.DMA((4,)),
            pltpu.VMEM((NCH, 2, 64, 16, 128), BF16),
            pltpu.VMEM((NCH, 2, 64, 16, 128), BF16),
            pltpu.VMEM((NCH, 64, 16, 128), BF16),
            pltpu.VMEM((NCH, 64, 16, 128), BF16),
            pltpu.VMEM((NCH, 3, 16, 16, 128), BF16),
            pltpu.VMEM((NCH, 16, 16, 128), BF16),
            pltpu.VMEM((NCH, 15, 16, 128), BF16),
            pltpu.SemaphoreType.DMA((6, NCH)),
            pltpu.SemaphoreType.DMA((6, NCH)),
        ],
        compiler_params=pltpu.CompilerParams(collective_id=0, has_side_effects=True, vmem_limit_bytes=60 * 2**20),
        name="nest_step",
    )(
        owner_count, parent, diffusion.reshape(1, chans), nest_state.reshape(rows, chans),
        nest_cotangent.reshape(rows, chans), tile_pos.reshape(1, own_tiles), w_in, w_out,
    )
    slab = lambda n: pl.BlockSpec((n, chans), lambda i: (i, 0))
    grad_in, grad_out, nest_grad, parent_out = pl.pallas_call(
        finish_kernel,
        grid=(NCH,),
        out_shape=[
            jax.ShapeDtypeStruct(w_in.shape, F32),
            jax.ShapeDtypeStruct(w_out.shape, F32),
            jax.ShapeDtypeStruct((rows, chans), BF16),
            jax.ShapeDtypeStruct((cells, chans), BF16),
        ],
        in_specs=[pl.BlockSpec((1, 2, 64, 16, 128), lambda i: (i, 0, 0, 0, 0)), slab(rows // NCH), slab(cells // NCH)],
        out_specs=[pl.BlockSpec((chans, CH), lambda i: (0, i)), slab(CH), slab(rows // NCH), slab(cells // NCH)],
        compiler_params=pltpu.CompilerParams(vmem_limit_bytes=60 * 2**20),
        name="finish",
    )(sums, nest_grad, parent_out)
    return (parent_out.reshape(parent.shape), nest_grad.reshape(nest_state.shape), grad_in, grad_out)


def solution(mesh):
    in_specs = (
        P("lat", "lon", None),
        P(),
        P(("lat", "lon"), None, None),
        P(("lat", "lon"), None, None),
        P(("lat", "lon")),
        P(("lat", "lon")),
        P(),
        P(),
    )
    out_specs = (P("lat", "lon", None), P(("lat", "lon"), None, None), P(), P())
    return jax.shard_map(local, mesh=mesh, in_specs=in_specs, out_specs=out_specs, check_vma=False)
```

```python
import math

import jax
import jax.numpy as jnp
from jax import lax
from jax.experimental import pallas as pl
from jax.experimental.pallas import tpu as pltpu
from jax.sharding import PartitionSpec as P

MESH = pl.DeviceIdType.MESH
F32 = jnp.float32
BF16 = jnp.bfloat16
NT = (((1,), (1,)), ((), ()))
TN = (((0,), (0,)), ((), ()))
G0 = math.sqrt(2.0 / math.pi)
G1 = G0 * 0.044715
CH = 256
NCH = 8
VMEM = pl.BlockSpec(memory_space=pltpu.VMEM)
PLANE = [(a, b) for a in range(4) for b in range(4) if a or b]


def gelu_pair(h, da):
    h2 = h * h
    s = 0.5 + 0.5 * jnp.tanh(h * (G0 + G1 * h2))
    act = h * s
    slope = s + act * (1.0 - s) * (2.0 * G0 + 6.0 * G1 * h2)
    return act.astype(BF16), (slope * da).astype(BF16)


class Place:
    def __init__(self):
        a, b = lax.axis_index("lat"), lax.axis_index("lon")
        self.x, self.y, self.z = lax.rem(a, 4), b // 2, a // 4
        self.core = lax.rem(b, 2)

    def to(self, dx, dy, dz):
        x, y, z = lax.rem(self.x + dx, 4), lax.rem(self.y + dy, 4), lax.rem(self.z + dz, 4)
        return (z * 4 + x, y * 2 + self.core)

    def partner(self):
        return (self.z * 4 + self.x, self.y * 2 + 1 - self.core)

    def side(self):
        return (self.z * 4 + self.x, lax.rem(self.y + 2 * self.core + 3, 4) * 2 + 1 - self.core)

    def lat(self, d):
        return (lax.rem(self.z * 4 + self.x + d, 16), self.y * 2 + self.core)

    def lon(self, d):
        return (self.z * 4 + self.x, lax.rem(self.y * 2 + self.core + d, 8))

    def axis(self, a):
        ex, ez = (2 - a) // 2, a // 2
        ey = 1 - ex - ez
        return ((ex, ey, ez), self.x * ex + self.y * ey + self.z * ez)


class Reduce:
    def __init__(self, part, full, rc, half, ra, qb, rp, send, recv):
        self.part, self.full, self.rc, self.half = part, full, rc, half
        self.ra, self.qb, self.rp, self.send, self.recv = ra, qb, rp, send, recv
        self.at = Place()

    def sets(self, c):
        a0 = lax.rem(c, 3)
        (e0, q) = self.at.axis(a0)
        (e1, u) = self.at.axis(lax.rem(a0 + 1, 3))
        (e2, v) = self.at.axis(lax.rem(a0 + 2, 3))
        return e0, e1, e2, q, u, v

    def copy(self, src, dst, stage, c, device):
        pltpu.make_async_remote_copy(
            src_ref=src, dst_ref=dst, send_sem=self.send.at[stage, c], recv_sem=self.recv.at[stage, c],
            device_id=device, device_id_type=MESH,
        ).start()

    def wait(self, ref, stage, c):
        pltpu.make_async_copy(ref, ref, self.recv.at[stage, c]).wait()

    def greet(self):
        barrier = pltpu.get_barrier_semaphore()
        others = [self.at.partner(), self.at.side()]
        for dx in range(4):
            for dy in range(4):
                for dz in range(4):
                    if (dx or dy or dz) and not (dx and dy and dz):
                        others.append(self.at.to(dx, dy, dz))
        for device in others:
            pl.semaphore_signal(barrier, inc=1, device_id=device, device_id_type=MESH)
        return barrier, len(others)

    def s0(self, c):
        self.copy(self.part.at[c, 1 - self.at.core], self.rc.at[c], 0, c, self.at.partner())

    def s1(self, c):
        e0, e1, e2, q, u, v = self.sets(c)
        self.wait(self.rc.at[c], 0, c)
        self.half[c] = (self.part[c, self.at.core].astype(F32) + self.rc[c].astype(F32)).astype(BF16)
        for d in (1, 2, 3):
            to = lax.rem(q + d, 4)
            self.copy(self.half.at[c, pl.ds(to * 16, 16)], self.ra.at[c, d - 1], 1, c, self.at.to(*(d * e for e in e0)))

    def s2(self, c):
        e0, e1, e2, q, u, v = self.sets(c)
        self.wait(self.ra.at[c], 1, c)
        mine = pl.ds(q * 16, 16)
        total = self.part[c, self.at.core, mine].astype(F32) + self.rc[c, mine].astype(F32)
        for d in range(3):
            total += self.ra[c, d].astype(F32)
        self.qb[c] = total.astype(BF16)
        for o, (d1, d2) in enumerate(PLANE):
            to = lax.rem(u + d1, 4) * 4 + lax.rem(v + d2, 4)
            self.copy(self.qb.at[c, to], self.rp.at[c, o], 2, c, self.at.to(*(d1 * f + d2 * g for f, g in zip(e1, e2))))

    def s3(self, c):
        e0, e1, e2, q, u, v = self.sets(c)
        self.wait(self.rp.at[c], 2, c)
        total = self.qb[c, u * 4 + v].astype(F32)
        for o in range(15):
            total += self.rp[c, o].astype(F32)
        spot = self.full.at[c, self.at.core, q * 16 + u * 4 + v]
        spot[...] = total.astype(BF16)
        for d1, d2 in PLANE:
            self.copy(spot, spot, 3, c, self.at.to(*(d1 * f + d2 * g for f, g in zip(e1, e2))))

    def s4(self, c):
        e0, e1, e2, q, u, v = self.sets(c)
        self.wait(self.rp.at[c], 3, c)
        spot = self.full.at[c, self.at.core, pl.ds(q * 16, 16)]
        for d in (1, 2, 3):
            self.copy(spot, spot, 4, c, self.at.to(*(d * e for e in e0)))

    def s5(self, c):
        self.wait(self.ra.at[c], 4, c)
        spot = self.full.at[c, self.at.core]
        self.copy(spot, spot, 5, c, self.at.partner())

    def s6(self, c, sums, out):
        self.wait(self.full.at[c, 1 - self.at.core], 5, c)
        for m in range(2):
            pltpu.make_async_copy(self.full.at[c, m], sums[m].at[c], out.at[c, m]).start()

    def drain(self, c):
        for stage, ref in enumerate((self.rc, self.ra, self.rp, self.rp, self.ra, self.rc)):
            pltpu.make_async_copy(ref.at[c], ref.at[c], self.send.at[stage, c]).wait()


def every(n, fn):
    def body(i, carry):
        fn(i)
        return carry

    lax.fori_loop(0, n, body, 0)


def rows_of(r, n):
    return pl.ds(pl.multiple_of(r * n, n), n)


def step_kernel(
    factor, count, parent_h, diff, nest_h, cot_h, pos, wi_h, wo_h,
    pout, dx, sums_in, sums_out,
    ext, edge, beside, sm, x, xT, cot, wi, wo, da, act, dh, fb, field_out, load, out, leaving, hs, hr, part, *scratch,
):
    r = Reduce(part, *scratch)
    at = r.at
    loads = [
        pltpu.make_async_copy(src, dst, load.at[i])
        for i, (src, dst) in enumerate(((parent_h, ext.at[pl.ds(1, 16)]), (cot_h, cot), (wo_h, wo), (nest_h, x), (wi_h, wi)))
    ]
    for c in loads[:3]:
        c.start()
    barrier, met = r.greet()
    live = count[0]

    loads[0].wait()
    for i in range(16):
        line = ext[1 + i].astype(F32)
        edge[0, i : i + 1] = line[0:1]
        edge[1, i : i + 1] = line[31:32]
    pl.semaphore_wait(barrier, met)

    def halo(i, src, dst, device):
        c = pltpu.make_async_remote_copy(
            src_ref=src, dst_ref=dst, send_sem=hs.at[i], recv_sem=hr.at[i], device_id=device, device_id_type=MESH
        )
        c.start()
        return c

    halos = [
        halo(0, ext.at[16], ext.at[0], at.lat(1)),
        halo(1, ext.at[1], ext.at[17], at.lat(15)),
        halo(2, edge.at[1], beside.at[0], at.lon(1)),
        halo(3, edge.at[0], beside.at[1], at.lon(7)),
    ]
    for c in loads[3:]:
        c.start()

    def mask(t):
        rows = rows_of(t, 256)
        index = lax.broadcasted_iota(jnp.int32, (256, 512), 0) + t * 256
        cot[rows, :] = jnp.where(index < live * 8, cot[rows, :].astype(F32), 0.0).astype(BF16)

    loads[1].wait()
    every(8, mask)
    loads[2].wait()
    da[...] = lax.dot_general(cot[...], wo[pl.ds(0, CH), :], NT, preferred_element_type=F32)
    cells = lax.broadcasted_iota(jnp.int32, (512, 256), 0)
    slots = lax.broadcasted_iota(jnp.int32, (512, 256), 1)
    hot = jnp.where((cells == pos[...]) & (slots < live), 1.0, 0.0).astype(BF16)
    for c in halos:
        c.wait()

    band = lax.axis_index("lat")

    @pl.when(band == 0)
    def _():
        ext[0] = jnp.zeros_like(ext[0])

    @pl.when(band == 15)
    def _():
        ext[17] = jnp.zeros_like(ext[17])

    west, east = beside[0], beside[1]
    column = lax.broadcasted_iota(jnp.int32, (32, 512), 0)
    rate = diff[...]
    for i in range(16):
        f = ext[1 + i].astype(F32)
        w = jnp.where(column == 0, west[i : i + 1], pltpu.roll(f, 1, 0))
        e = jnp.where(column == 31, east[i : i + 1], pltpu.roll(f, 31, 0))
        near = ext[i].astype(F32) + ext[2 + i].astype(F32) + w + e - 4.0 * f
        sm[32 * i : 32 * i + 32] = f + rate * near
    field = sm[...]
    high = field.astype(BF16)
    low = (field - high.astype(F32)).astype(BF16)
    context = lax.dot_general(hot, high, TN, preferred_element_type=F32)
    context += lax.dot_general(hot, low, TN, preferred_element_type=F32)
    loads[3].wait()
    for t in range(4):
        rows = pl.ds(t * 512, 512)
        wide = jnp.broadcast_to(context[64 * t : 64 * t + 64, None, :], (64, 8, 512)).reshape(512, 512)
        x[rows, :] = (x[rows, :].astype(F32) + wide).astype(BF16)
    loads[4].wait()
    xT[...] = x[...].T

    def tiles(j, first):
        cols = rows_of(j, CH)

        h = jnp.dot(x[...], wi[:, cols], preferred_element_type=F32)
        d = da[...] if first else lax.dot_general(cot[...], wo[cols, :], NT, preferred_element_type=F32)
        a, d = gelu_pair(h, d)
        act[:, cols] = a
        dh[:, cols] = d

    def grads(j):
        cols = rows_of(j, CH)
        g = jnp.dot(xT[...], dh[:, cols], preferred_element_type=F32) * factor
        for k in range(2):
            part[j, 0, 32 * k : 32 * k + 32] = g[:, 128 * k : 128 * k + 128].astype(BF16).reshape(32, 16, 128)
        g = lax.dot_general(act[:, cols], cot[...], TN, preferred_element_type=F32) * factor
        for k in range(4):
            part[j, 1, 16 * k : 16 * k + 16] = g[:, 128 * k : 128 * k + 128].astype(BF16).reshape(16, 16, 128)

    def rest(t):
        rows = rows_of(t, 256)
        d = lax.dot_general(dh[rows, :], wi[...], NT, preferred_element_type=F32)
        cot[rows, :] = (d + cot[rows, :].astype(F32)).astype(BF16)
        pltpu.make_async_copy(cot.at[rows], dx.at[rows], out.at[t]).start()
        o = jnp.dot(act[rows, :], wo[...], preferred_element_type=F32) + x[rows, :].astype(F32)
        fb[rows_of(t, 32), :] = jnp.mean(o.reshape(32, 8, 512), axis=1).astype(BF16)

    def stages(s, *pairs):
        for stage, delay in pairs:
            c = s - delay

            @pl.when((c >= 0) & (c < NCH))
            def _():
                stage(c)

    odd = ((r.s1, 1), (r.s3, 4), (r.s5, 7),)
    even = ((r.s2, 2), (r.s4, 5), ((lambda c: r.s6(c, (sums_in, sums_out), leaving)), 7),)
    tiles(0, True)

    def slot(s):
        @pl.when(s > 0)
        def _():
            tiles(s, False)

        stages(s, *odd)
        grads(s)
        r.s0(s)
        stages(s, *even)

    every(NCH, slot)

    def late(i):
        @pl.when(i < 4)
        def _():
            rest(2 * i)

        stages(i + 8, *odd)

        @pl.when(i < 4)
        def _():
            rest(2 * i + 1)

        @pl.when(i == 4)
        def _():
            field_out[...] = (sm[...] + jnp.dot(hot, fb[...], preferred_element_type=F32)).astype(BF16)
            pltpu.make_async_copy(field_out, pout, out.at[16]).start()

        stages(i + 8, *even)

    every(7, late)
    every(NCH, r.drain)

    def leave(t):
        rows = rows_of(t, 256)
        pltpu.make_async_copy(cot.at[rows], dx.at[rows], out.at[t]).wait()
        pltpu.make_async_copy(r.full.at[t, 0], sums_in.at[t], leaving.at[t, 0]).wait()
        pltpu.make_async_copy(r.full.at[t, 1], sums_out.at[t], leaving.at[t, 1]).wait()

    every(8, leave)
    pltpu.make_async_copy(field_out, pout, out.at[16]).wait()


def finish_kernel(sums_in, sums_out, gi, go):
    for k in range(2):
        gi[:, 128 * k : 128 * k + 128] = sums_in[0, 32 * k : 32 * k + 32].reshape(512, 128).astype(F32)
    for k in range(4):
        go[:, 128 * k : 128 * k + 128] = sums_out[0, 16 * k : 16 * k + 16].reshape(256, 128).astype(F32)


def local(parent, diffusion, nest_state, nest_cotangent, owner_count, tile_pos, w_in, w_out):
    blat, blon, chans = parent.shape
    own_tiles, tile_rows = (nest_state.shape[0], nest_state.shape[1])
    rows, cells, hidden = own_tiles * tile_rows, blat * blon, w_in.shape[1]
    devices = lax.axis_size(("lat", "lon"))
    factor = 1.0 / math.sqrt(own_tiles * devices // 4 * tile_rows)
    hbm = pl.BlockSpec(memory_space=pl.ANY)
    parent_out, nest_grad, sums_in, sums_out = pl.pallas_call(
        lambda *refs: step_kernel(factor, *refs),
        out_shape=[
            jax.ShapeDtypeStruct((cells, chans), BF16),
            jax.ShapeDtypeStruct((rows, chans), BF16),
            jax.ShapeDtypeStruct((NCH, 64, 16, 128), BF16),
            jax.ShapeDtypeStruct((NCH, 64, 16, 128), BF16),
        ],
        in_specs=[pl.BlockSpec(memory_space=pltpu.SMEM), hbm, VMEM, hbm, hbm, VMEM, hbm, hbm],
        out_specs=[hbm] * 4,
        scratch_shapes=[
            pltpu.VMEM((blat + 2, blon, chans), BF16),
            pltpu.VMEM((2, blat, chans), F32),
            pltpu.VMEM((2, blat, chans), F32),
            pltpu.VMEM((cells, chans), F32),
            pltpu.VMEM((rows, chans), BF16),
            pltpu.VMEM((chans, rows), BF16),
            pltpu.VMEM((rows, chans), BF16),
            pltpu.VMEM(w_in.shape, BF16),
            pltpu.VMEM(w_out.shape, BF16),
            pltpu.VMEM((rows, CH), F32),
            pltpu.VMEM((rows, hidden), BF16),
            pltpu.VMEM((rows, hidden), BF16),
            pltpu.VMEM((own_tiles, chans), BF16),
            pltpu.VMEM((cells, chans), BF16),
            pltpu.SemaphoreType.DMA((5,)),
            pltpu.SemaphoreType.DMA((17,)),
            pltpu.SemaphoreType.DMA((NCH, 2)),
            pltpu.SemaphoreType.DMA((4,)),
            pltpu.SemaphoreType.DMA((4,)),
            pltpu.VMEM((NCH, 2, 64, 16, 128), BF16),
            pltpu.VMEM((NCH, 2, 64, 16, 128), BF16),
            pltpu.VMEM((NCH, 64, 16, 128), BF16),
            pltpu.VMEM((NCH, 64, 16, 128), BF16),
            pltpu.VMEM((NCH, 3, 16, 16, 128), BF16),
            pltpu.VMEM((NCH, 16, 16, 128), BF16),
            pltpu.VMEM((NCH, 15, 16, 128), BF16),
            pltpu.SemaphoreType.DMA((6, NCH)),
            pltpu.SemaphoreType.DMA((6, NCH)),
        ],
        compiler_params=pltpu.CompilerParams(collective_id=0, has_side_effects=True, vmem_limit_bytes=60 * 2**20),
        name="nest_step",
    )(
        owner_count, parent, diffusion.reshape(1, chans), nest_state.reshape(rows, chans),
        nest_cotangent.reshape(rows, chans), tile_pos.reshape(1, own_tiles), w_in, w_out,
    )
    slab = lambda n: pl.BlockSpec((n, chans), lambda i: (i, 0))
    grad_in, grad_out = pl.pallas_call(
        finish_kernel,
        grid=(NCH,),
        out_shape=[jax.ShapeDtypeStruct(w_in.shape, F32), jax.ShapeDtypeStruct(w_out.shape, F32)],
        in_specs=[pl.BlockSpec((1, 64, 16, 128), lambda i: (i, 0, 0, 0))] * 2,
        out_specs=[pl.BlockSpec((chans, CH), lambda i: (0, i)), slab(CH)],
        compiler_params=pltpu.CompilerParams(vmem_limit_bytes=8 * 2**20),
        name="finish",
    )(sums_in, sums_out)
    return (parent_out.reshape(parent.shape), nest_grad.reshape(nest_state.shape), grad_in, grad_out)


def solution(mesh):
    in_specs = (
        P("lat", "lon", None),
        P(),
        P(("lat", "lon"), None, None),
        P(("lat", "lon"), None, None),
        P(("lat", "lon")),
        P(("lat", "lon")),
        P(),
        P(),
    )
    out_specs = (P("lat", "lon", None), P(("lat", "lon"), None, None), P(), P())
    return jax.shard_map(local, mesh=mesh, in_specs=in_specs, out_specs=out_specs, check_vma=False)
```
